32 devices in a mesh: groups: 2 (over x), section: 2 (over core), expert: 8 (over z, y).
Axes of the slice: x: 2, y: 2, z: 4, core: 2. Of those that a mesh axis runs over, the one named last changes fastest.
Arguments:
- token_rows: bfloat16 [2, 256, 3072], P('section', ('groups', 'expert')), parts along dimension 1, may hold values from -36 to 36
- norm_gain: float32 [2, 3072], P('section'), may hold values from 0.1 to 1.9
- router: float32 [2, 3072, 4], P('section'), may hold values from -0.109375 to 0.109375
- w_gate: bfloat16 [2, 8, 3072, 4096], P('section', 'expert'), may hold values from -0.109375 to 0.109375
- w_up: bfloat16 [2, 8, 3072, 4096], P('section', 'expert'), may hold values from -0.109375 to 0.109375
- w_down: bfloat16 [2, 8, 4096, 3072], P('section', 'expert'), may hold values from -0.0625 to 0.0625
- routes: int32 [2, 256, 2], P('section', 'groups'), parts along dimension 1, may hold values from 0 to 3, all different within a row; in each aligned block of 16 rows (0 to 15, 16 to 31, ..., all dimensions but the last counted through in order) at most 16 rows name the same one
Outputs:
- next_rows: bfloat16 [2, 256, 3072], P('section', ('groups', 'expert')), parts along dimension 1
The draws below stay inside these ranges and needn't reach their ends.
There are 2 independent parts, one for each index of `groups`. The reference program is written for one: setup_inputs(seed, part) draws one part's arguments, and reference() takes and returns one part's arrays. A program takes and returns all parts, laid end to end along the dimension named above; an argument that names none is the same for every part. Nothing has to cross between parts.
Inputs may be any that keep to these rules, and one draw needn't show every extreme that they name: `routes`: the two experts of a row differ, and every expert is named by some row.
All inputs are finite; a program needn't handle non-finite values.
Results may differ from the reference program's by a relative error of at most 0.0026.
Values may be sent and summed in bfloat16 or wider, within the bound.
A program may use at most 192 MiB of HBM per device.

```python
import math
import jax
import jax.numpy as jnp
import numpy as np
from jax import lax

D = 3072
FF = 8192
EXPERTS = 4
ROWS_DEV = 16
SECTIONS = 2
SLICES = 2
FF_DEV = 4096
TOKENS = 128


def draw_token_rows(key, part):
    key_base, key_row, key_col = jax.random.split(key, 3)
    shape_all = (SECTIONS, TOKENS, D)
    base_value = jnp.clip(jax.random.normal(key_base, shape_all, jnp.float32), -4.0, 4.0)
    log_low = math.log(0.3)
    log_high = math.log(3.0)
    row_scale = jnp.exp(jax.random.uniform(key_row, (SECTIONS, TOKENS, 1), jnp.float32, log_low, log_high))
    col_scale = jnp.exp(jax.random.uniform(key_col, (SECTIONS, 1, D), jnp.float32, log_low, log_high))
    return jnp.clip(base_value * row_scale * col_scale, -36.0, 36.0).astype(jnp.bfloat16)


def level_of(own_key, dims, cuts, smallest, high):
    level = 1.0
    for position, parts in cuts:
        heights = jax.random.uniform(jax.random.fold_in(jax.random.fold_in(own_key, 6), position), (parts,), jnp.float32, smallest / len(cuts), high / len(cuts))
        level = level * jnp.repeat(jnp.exp(heights), dims[position] // parts).reshape((-1,) + (1,) * (len(dims) - 1 - position))
    return level


def routed_block(key, own, number, rows, amount, top, reach, skew):
    order = jax.random.permutation(key, amount)
    heavy_load, usual = shares(amount, rows * top, reach, skew, True), shares(amount, rows * top, reach, skew, False)
    places = jnp.arange(amount)

    def named(sizes, offset_by):
        used = int((sizes > 0).sum())
        fixed = max(1, used // 4)
        shifted = fixed + (places - fixed + offset_by * (used - fixed)) % max(1, amount - fixed)
        return jnp.zeros((amount,), jnp.int32).at[order[jnp.where(places < fixed, places, shifted)]].set(jnp.asarray(sizes, jnp.int32))

    sizes = jnp.where(number % 4 == 0, named(heavy_load, number // 4), named(usual, number - number // 4 - 1))
    mixed = jax.random.permutation(jax.random.fold_in(own, 3), amount)
    source_of, receiver = mixed[0:amount // 2 * 2:2], mixed[1:amount // 2 * 2:2]
    room = jnp.minimum(sizes[source_of] - 1, reach - sizes[receiver]) // 2
    room = jnp.where((source_of == order[0]) | (receiver == order[0]) | (sizes[receiver] == 0), 0, jnp.maximum(room, 0))
    shifted = jax.random.randint(jax.random.fold_in(own, 4), (amount // 2,), 0, 1 << 20) % (room + 1)
    sizes = sizes.at[source_of].add(-shifted).at[receiver].add(shifted)
    labels = jnp.searchsorted(jnp.cumsum(sizes), jnp.arange(rows * top), side="right").astype(jnp.int32)
    table = labels.reshape(top, rows).T
    table = table[jax.random.permutation(jax.random.fold_in(own, 1), rows)]
    offset_by = jax.random.randint(jax.random.fold_in(own, 2), (rows, 1), 0, top)
    return jnp.take_along_axis(table, (jnp.arange(top)[None, :] + offset_by) % top, axis=1)


def shares(count, total, most, skew, full):
    loads = [(1 << 20) // math.isqrt(grade ** skew) + 1 for grade in range(1, count + 1)]
    largest = most if full else min(most, max(-(-total // count), total * loads[0] // sum(loads)))
    least = 1 if total - largest >= count - 1 else 0
    given, surplus = [largest] + [least] * (count - 1), total - largest - least * (count - 1)
    while surplus > 0:
        movable = [i for i in range(1, count) if given[i] < largest] or [i for i in range(1, count) if given[i] < most]
        whole, remaining = sum([loads[i] for i in movable]), surplus
        for i in movable:
            addition = min(most - given[i], max(1, remaining * loads[i] // whole), surplus)
            given[i] = given[i] + addition
            surplus = surplus - addition
    return np.array(given)


def bell_draw(stream_key, extent, deviation, limit, shards=(), kind=jnp.bfloat16):
    array = jax.random.normal(stream_key, extent, jnp.float32) * deviation
    if len(shards) > 0:
        array = level_of(stream_key, extent, shards, -0.22, 0.18) * array
    return jnp.clip(array, min=-limit, max=limit).astype(kind)


def setup_inputs(seed: int = 0, part: int = 0) -> dict:
    splits = jax.random.split(jax.random.key(seed), 8)
    own_keys = jax.random.split(jax.random.fold_in(splits[7], part), 8)
    token_rows = draw_token_rows(jax.random.fold_in(jax.random.fold_in(splits[7], part), 71), part)
    norm_gain = jnp.clip(1.0 + 0.18 * jax.random.normal(splits[1], (SECTIONS, D), jnp.float32), 0.1, 1.9)
    router = bell_draw(splits[2], (SECTIONS, D, EXPERTS), D ** -0.5, 0.109375, ((0, 2),), jnp.float32)
    w_gate = bell_draw(splits[3], (SECTIONS, SLICES * EXPERTS, D, FF_DEV), D ** -0.5, 0.109375, ((0, 2), (1, 8)))
    w_up = bell_draw(splits[4], (SECTIONS, SLICES * EXPERTS, D, FF_DEV), D ** -0.5, 0.109375, ((0, 2), (1, 8)))
    w_down = bell_draw(splits[5], (SECTIONS, SLICES * EXPERTS, FF_DEV, D), FF ** -0.5, 0.0625, ((0, 2), (1, 8)))
    routes_keys = jax.random.split(jax.random.fold_in(own_keys[6], 1), SECTIONS * TOKENS // ROWS_DEV)
    routes_turns = jax.random.permutation(jax.random.fold_in(own_keys[6], 3), SECTIONS * TOKENS // ROWS_DEV)
    routes = jax.vmap(lambda own, number: routed_block(jax.random.fold_in(own_keys[6], 2), own, number, ROWS_DEV, EXPERTS, 2, ROWS_DEV, 2))(routes_keys, routes_turns).reshape((SECTIONS, TOKENS, 2))
    return {"token_rows": token_rows, "norm_gain": norm_gain, "router": router, "w_gate": w_gate, "w_up": w_up, "w_down": w_down, "routes": routes}


epsilon = 1e-05

def normalize(residual, gain):
    values = residual.astype(jnp.float32)
    inv_rms = lax.rsqrt(lax.optimization_barrier(jnp.mean(values * values, axis=-1, keepdims=True)) + epsilon)
    return (values * inv_rms * gain).astype(jnp.bfloat16)

def mixing_weights(normed, router_cols, pair):
    logits = jnp.dot(normed.astype(jnp.float32), router_cols, precision=lax.Precision.HIGHEST)
    expert_ids = jnp.arange(router_cols.shape[1], dtype=jnp.int32)
    first_hit = (pair[:, 0:1] == expert_ids[None, :]).astype(jnp.float32)
    second_hit = (pair[:, 1:2] == expert_ids[None, :]).astype(jnp.float32)
    first_logit = lax.optimization_barrier(jnp.sum(logits * first_hit, axis=1))
    second_logit = lax.optimization_barrier(jnp.sum(logits * second_hit, axis=1))
    first_gate = 1.0 / (1.0 + jnp.exp(second_logit - first_logit))
    second_gate = 1.0 / (1.0 + jnp.exp(first_logit - second_logit))
    member = first_hit + second_hit
    mixing = first_hit * first_gate[:, None] + second_hit * second_gate[:, None]
    return (member, mixing)

def moe_layer(residual, gain, router_cols, pair, gate_all, up_all, down_all):
    normed = normalize(residual, gain)
    mixing = mixing_weights(normed, router_cols, pair)[1]
    branch = jnp.zeros(residual.shape, jnp.float32)
    for expert in range(EXPERTS):
        gate_full = jnp.transpose(gate_all.reshape(SLICES, EXPERTS, D, FF_DEV)[:, expert], (1, 0, 2)).reshape(D, FF)
        up_full = jnp.transpose(up_all.reshape(SLICES, EXPERTS, D, FF_DEV)[:, expert], (1, 0, 2)).reshape(D, FF)
        down_full = down_all.reshape(SLICES, EXPERTS, FF_DEV, D)[:, expert].reshape(FF, D)
        gate_proj = jnp.dot(normed, gate_full, preferred_element_type=jnp.float32)
        up_proj = jnp.dot(normed, up_full, preferred_element_type=jnp.float32)
        hidden = (jax.nn.silu(gate_proj) * up_proj).astype(jnp.bfloat16)
        expert_out = jnp.dot(hidden, down_full, preferred_element_type=jnp.float32)
        branch = branch + mixing[:, expert:expert + 1] * expert_out
    return (residual.astype(jnp.float32) + branch).astype(jnp.bfloat16)

def reference(token_rows, norm_gain, router, w_gate, w_up, w_down, routes):
    results = [moe_layer(token_rows[section_id], norm_gain[section_id], router[section_id], routes[section_id], w_gate[section_id], w_up[section_id], w_down[section_id]) for section_id in range(SECTIONS)]
    return jnp.roll(jnp.stack(results), 1, axis=0)
```

```python
import functools

import jax
import jax.numpy as jnp
from jax import lax
from jax.experimental import pallas as pl
from jax.experimental.pallas import tpu as pltpu
from jax.sharding import PartitionSpec as P

epsilon = 1e-05
MESH = pl.DeviceIdType.MESH


def each(count, start, body):
    if count <= 8:
        for i in range(start, count):
            body(i)
    else:
        def step(i, carry):
            body(i)
            return carry

        lax.fori_loop(start, count, step, 0)


def kernel(
    cfg,
    x_ref, gain_ref, router_ref, routes_ref, gate_hbm, up_hbm, down_hbm,
    out_ref,
    gathered, gate_buf, up_buf, down_buf, gate_acc, up_acc, hidden, mixing,
    send_y, own, recv_y, send_z, recv_z, resid,
    gate_sem, up_sem, down_sem, res_sem, az_send, az_recv, ay_send, ay_recv,
    ry_send, ry_recv, rz_send, rz_recv,
):
    nz, rows, kc, nk, slots, ff, ft, nc, cw, experts = cfg
    half = nz * rows
    position = lax.axis_index("expert")
    section = lax.axis_index("section")
    z, y = position // 2, position % 2
    expert = position % experts
    other = 1 - section

    def ring(value):
        return lax.rem(value + nz, nz)

    def rows_at(start):
        return pl.ds(pl.multiple_of(start * rows, rows), rows)

    def load_gate(k):
        return pltpu.make_async_copy(
            gate_hbm.at[0, 0, pl.ds(k * kc, kc), :], gate_buf.at[k % slots], gate_sem.at[k % slots])

    def load_up(k):
        return pltpu.make_async_copy(
            up_hbm.at[0, 0, pl.ds(k * kc, kc), :], up_buf.at[k % slots], up_sem.at[k % slots])

    def load_down(c):
        return pltpu.make_async_copy(
            down_hbm.at[0, 0, :, pl.ds(pl.multiple_of(c * cw, cw), cw)], down_buf.at[c], down_sem.at[c])

    def along_z(k, j):
        return pltpu.make_async_remote_copy(
            src_ref=gathered.at[k, rows_at(z), :], dst_ref=gathered.at[k, rows_at(z), :],
            send_sem=az_send.at[k, j], recv_sem=az_recv.at[k, j],
            device_id={"expert": ring(z + j) * 2 + y}, device_id_type=MESH)

    def from_z(k, j):
        src = rows_at(ring(z - j))
        return pltpu.make_async_remote_copy(
            src_ref=gathered.at[k, src, :], dst_ref=gathered.at[k, src, :],
            send_sem=az_send.at[k, j], recv_sem=az_recv.at[k, j],
            device_id={"expert": ring(z + j) * 2 + y}, device_id_type=MESH)

    def along_y(k, j):
        row = ring(z - j)
        return pltpu.make_async_remote_copy(
            src_ref=gathered.at[k, rows_at(row), :], dst_ref=gathered.at[k, rows_at(nz + row), :],
            send_sem=ay_send.at[k, j], recv_sem=ay_recv.at[k, j],
            device_id={"expert": z * 2 + 1 - y}, device_id_type=MESH)

    def reduce_y(c):
        return pltpu.make_async_remote_copy(
            src_ref=send_y.at[c], dst_ref=recv_y.at[c],
            send_sem=ry_send.at[c], recv_sem=ry_recv.at[c],
            device_id={"expert": z * 2 + 1 - y}, device_id_type=MESH)

    def reduce_z(c, j):
        row = ring(z + j)
        return pltpu.make_async_remote_copy(
            src_ref=send_z.at[c, rows_at(row), :], dst_ref=recv_z.at[c, j],
            send_sem=rz_send.at[c, j], recv_sem=rz_recv.at[c, j],
            device_id={"section": other, "expert": row * 2 + y}, device_id_type=MESH)

    for k in range(min(slots, nk)):
        load_gate(k).start()
        load_up(k).start()

    barrier = pltpu.get_barrier_semaphore()

    def greet_z(j):
        pl.semaphore_signal(
            barrier, inc=1, device_id={"expert": ring(z + j) * 2 + y}, device_id_type=MESH)

    def greet_other(j):
        pl.semaphore_signal(
            barrier, inc=1, device_id={"section": other, "expert": ring(z + j) * 2 + y},
            device_id_type=MESH)

    each(nz, 1, greet_z)
    each(nz, 0, greet_other)
    pl.semaphore_signal(
        barrier, inc=1, device_id={"expert": z * 2 + 1 - y}, device_id_type=MESH)

    values = x_ref[0].astype(jnp.float32)
    inv_rms = lax.rsqrt(jnp.mean(values * values, axis=-1, keepdims=True) + epsilon)
    for k in range(nk):
        cols = slice(k * kc, (k + 1) * kc)
        gathered[k, rows_at(z), :] = (values[:, cols] * inv_rms * gain_ref[:, cols]).astype(jnp.bfloat16)

    pl.semaphore_wait(barrier, 2 * nz)
    for k in range(nk):
        along_y(k, 0).start()
        each(nz, 1, lambda j: along_z(k, j).start())
    res_copy = pltpu.make_async_remote_copy(
        src_ref=x_ref, dst_ref=resid, send_sem=res_sem.at[0], recv_sem=res_sem.at[1],
        device_id={"section": other}, device_id_type=MESH)
    res_copy.start()

    def forward(k):
        def one(j):
            from_z(k, j).wait_recv()
            along_y(k, j).start()

        each(nz, 1, one)

    forward(0)
    for k in range(nk):
        if k + 1 < nk:
            forward(k + 1)
        each(nz, 0, lambda j: along_y(k, j).wait_recv())
        load_gate(k).wait()
        load_up(k).wait()
        slot = k % slots

        def tile(t, carry):
            cols = pl.ds(pl.multiple_of(t * ft, ft), ft)
            lhs = gathered[k]
            gate = jnp.dot(lhs, gate_buf[slot, :, cols], preferred_element_type=jnp.float32)
            up = jnp.dot(lhs, up_buf[slot, :, cols], preferred_element_type=jnp.float32)
            if k > 0:
                gate = gate + gate_acc[:, cols]
                up = up + up_acc[:, cols]
            if k < nk - 1:
                gate_acc[:, cols] = gate
                up_acc[:, cols] = up
            else:
                hidden[:, cols] = (gate / (1.0 + jnp.exp(-gate)) * up).astype(jnp.bfloat16)
            return carry

        lax.fori_loop(0, ff // ft, tile, 0)
        if k + slots < nk:
            load_gate(k + slots).start()
            load_up(k + slots).start()
        if k == max(nk - slots - 1, 0):
            for c in range(nc):
                load_down(c).start()

    def mix(i, carry):
        side, row = i // nz, lax.rem(i, nz)
        source = row * 2 + jnp.where(side == 0, y, 1 - y)
        here = rows_at(i)
        pair = routes_ref[rows_at(source), :]
        first, second = pair[:, 0:1], pair[:, 1:2]
        first_logit = jnp.zeros((rows, 1), jnp.float32)
        second_logit = jnp.zeros((rows, 1), jnp.float32)
        for e in range(experts):
            total = jnp.zeros((rows, kc), jnp.float32)
            for k in range(nk):
                total = total + gathered[k, here, :].astype(jnp.float32) * router_ref[
                    e:e + 1, k * kc:(k + 1) * kc]
            logit = jnp.sum(total, axis=-1, keepdims=True)
            first_logit = jnp.where(first == e, logit, first_logit)
            second_logit = jnp.where(second == e, logit, second_logit)
        first_gate = 1.0 / (1.0 + jnp.exp(second_logit - first_logit))
        second_gate = 1.0 / (1.0 + jnp.exp(first_logit - second_logit))
        weight = jnp.where(first == expert, first_gate, 0.0) + jnp.where(
            second == expert, second_gate, 0.0)
        mixing[here, :] = jnp.broadcast_to(weight, (rows, 128))
        return carry

    lax.fori_loop(0, 2 * nz, mix, 0)

    def second_stage(c):
        reduce_y(c).wait_recv()
        send_z[c] = (own[c] + recv_y[c].astype(jnp.float32)).astype(jnp.bfloat16)
        each(nz, 0, lambda j: reduce_z(c, j).start())

    lag = 2

    def down(c, carry):
        load_down(c).wait()
        part = jnp.dot(hidden[...], down_buf[c], preferred_element_type=jnp.float32)
        part = part * mixing[:, 0:1]
        send_y[c] = part[half:].astype(jnp.bfloat16)
        reduce_y(c).start()
        own[c] = part[:half]

        @pl.when(c >= lag)
        def _():
            second_stage(c - lag)

        return carry

    lax.fori_loop(0, nc, down, 0)
    for c in range(nc - lag, nc):
        second_stage(c)
    res_copy.wait_recv()
    for c in range(nc):
        cols = slice(c * cw, (c + 1) * cw)
        each(nz, 0, lambda j: reduce_z(c, j).wait_recv())
        branch = jnp.sum(recv_z[c].astype(jnp.float32), axis=0)
        out_ref[0, :, cols] = (resid[0, :, cols].astype(jnp.float32) + branch).astype(jnp.bfloat16)

    res_copy.wait_send()
    for k in range(nk):
        each(nz, 1, lambda j: along_z(k, j).wait_send())
        each(nz, 0, lambda j: along_y(k, j).wait_send())

    def drain(c, carry):
        reduce_y(c).wait_send()
        each(nz, 0, lambda j: reduce_z(c, j).wait_send())
        return carry

    lax.fori_loop(0, nc, drain, 0)


def body(token_rows, norm_gain, router, w_gate, w_up, w_down, routes):
    _, rows, features = token_rows.shape
    ff = w_gate.shape[3]
    experts = router.shape[2]
    nz = lax.axis_size("expert") // 2
    total = 2 * nz * rows
    half = nz * rows
    kc, cw = 512, 256
    nk, nc = features // kc, features // cw
    slots = 3
    ft = min(512, ff)
    cfg = (nz, rows, kc, nk, slots, ff, ft, nc, cw, experts)
    vmem = pl.BlockSpec(memory_space=pltpu.VMEM)
    hbm = pl.BlockSpec(memory_space=pl.ANY)
    bf16, f32 = jnp.bfloat16, jnp.float32
    dma = pltpu.SemaphoreType.DMA
    return pl.pallas_call(
        functools.partial(kernel, cfg),
        out_shape=jax.ShapeDtypeStruct((1, rows, features), bf16),
        in_specs=[vmem] * 4 + [hbm] * 3,
        out_specs=vmem,
        scratch_shapes=[
            pltpu.VMEM((nk, total, kc), bf16),
            pltpu.VMEM((slots, kc, ff), bf16),
            pltpu.VMEM((slots, kc, ff), bf16),
            pltpu.VMEM((nc, ff, cw), bf16),
            pltpu.VMEM((total, ff), f32),
            pltpu.VMEM((total, ff), f32),
            pltpu.VMEM((total, ff), bf16),
            pltpu.VMEM((total, 128), f32),
            pltpu.VMEM((nc, half, cw), bf16),
            pltpu.VMEM((nc, half, cw), f32),
            pltpu.VMEM((nc, half, cw), bf16),
            pltpu.VMEM((nc, half, cw), bf16),
            pltpu.VMEM((nc, nz, rows, cw), bf16),
            pltpu.VMEM((1, rows, features), bf16),
            dma((slots,)), dma((slots,)), dma((nc,)), dma((2,)),
            dma((nk, nz)), dma((nk, nz)), dma((nk, nz)), dma((nk, nz)),
            dma((nc,)), dma((nc,)), dma((nc, nz)), dma((nc, nz)),
        ],
        compiler_params=pltpu.CompilerParams(
            collective_id=0, has_side_effects=True, vmem_limit_bytes=62 * 2**20),
    )(token_rows, norm_gain, router[0].T, routes[0], w_gate, w_up, w_down)


def solution(mesh):
    in_specs = (
        P("section", ("groups", "expert"), None),
        P("section", None),
        P("section", None, None),
        P("section", "expert", None, None),
        P("section", "expert", None, None),
        P("section", "expert", None, None),
        P("section", "groups", None),
    )
    out_specs = P("section", ("groups", "expert"), None)
    return jax.shard_map(body, mesh=mesh, in_specs=in_specs, out_specs=out_specs, check_vma=False)
```

```python
import functools

import jax
import jax.numpy as jnp
from jax import lax
from jax.experimental import pallas as pl
from jax.experimental.pallas import tpu as pltpu
from jax.sharding import PartitionSpec as P

epsilon = 1e-05
MESH = pl.DeviceIdType.MESH


def each(count, start, body):
    if count <= 8:
        for i in range(start, count):
            body(i)
    else:
        def step(i, carry):
            body(i)
            return carry

        lax.fori_loop(start, count, step, 0)


def kernel(
    cfg,
    x_hbm, gain_hbm, router_hbm, routes_ref, gate_hbm, up_hbm, down_hbm,
    out_ref,
    x_ref, gain_ref, router_ref, first_col, second_col, logits,
    gathered, gate_buf, up_buf, down_buf, gate_acc, up_acc, hidden, mixing,
    send_y, own, recv_y, send_z, recv_z, resid,
    small_sem, gate_sem, up_sem, down_sem, res_sem, az_send, az_recv, ay_send, ay_recv,
    ry_send, ry_recv, rz_send, rz_recv,
):
    nz, rows, kc, nk, per, slots, ff, ft, nc, cw, lag, experts = cfg
    na, ac = nk // per, kc * per
    tokens = 2 * nz * rows
    half = nz * rows
    position = lax.axis_index("expert")
    section = lax.axis_index("section")
    z, y = position // 2, position % 2
    expert = position % experts
    other = 1 - section

    def ring(value):
        return lax.rem(value + nz, nz)

    def rows_at(start):
        return pl.ds(pl.multiple_of(start * rows, rows), rows)

    def load_gate(k):
        return pltpu.make_async_copy(
            gate_hbm.at[0, 0, pl.ds(k * kc, kc), :], gate_buf.at[k % slots], gate_sem.at[k % slots])

    def load_up(k):
        return pltpu.make_async_copy(
            up_hbm.at[0, 0, pl.ds(k * kc, kc), :], up_buf.at[k % slots], up_sem.at[k % slots])

    def load_down(c):
        return pltpu.make_async_copy(
            down_hbm.at[0, 0, :, pl.ds(pl.multiple_of(c * cw, cw), cw)], down_buf.at[c], down_sem.at[c])

    def along_z(k, j):
        return pltpu.make_async_remote_copy(
            src_ref=gathered.at[k, rows_at(z), :], dst_ref=gathered.at[k, rows_at(z), :],
            send_sem=az_send.at[k, j], recv_sem=az_recv.at[k, j],
            device_id={"expert": ring(z + j) * 2 + y}, device_id_type=MESH)

    def from_z(k, j):
        src = rows_at(ring(z - j))
        return pltpu.make_async_remote_copy(
            src_ref=gathered.at[k, src, :], dst_ref=gathered.at[k, src, :],
            send_sem=az_send.at[k, j], recv_sem=az_recv.at[k, j],
            device_id={"expert": ring(z + j) * 2 + y}, device_id_type=MESH)

    def along_y(k, j):
        row = ring(z - j)
        return pltpu.make_async_remote_copy(
            src_ref=gathered.at[k, rows_at(row), :], dst_ref=gathered.at[k, rows_at(nz + row), :],
            send_sem=ay_send.at[k, j], recv_sem=ay_recv.at[k, j],
            device_id={"expert": z * 2 + 1 - y}, device_id_type=MESH)

    def reduce_y(c):
        return pltpu.make_async_remote_copy(
            src_ref=send_y.at[c], dst_ref=recv_y.at[c],
            send_sem=ry_send.at[c], recv_sem=ry_recv.at[c],
            device_id={"expert": z * 2 + 1 - y}, device_id_type=MESH)

    def reduce_z(c, j):
        row = ring(z + j)
        return pltpu.make_async_remote_copy(
            src_ref=send_z.at[c, rows_at(row), :], dst_ref=recv_z.at[c, j],
            send_sem=rz_send.at[c, j], recv_sem=rz_recv.at[c, j],
            device_id={"section": other, "expert": row * 2 + y}, device_id_type=MESH)

    small = [
        pltpu.make_async_copy(src, dst, small_sem.at[i])
        for i, (src, dst) in enumerate(
            ((x_hbm, x_ref), (gain_hbm, gain_ref), (router_hbm, router_ref)))
    ]
    for copy in small:
        copy.start()
    for k in range(slots - 1):
        load_gate(k).start()
        load_up(k).start()

    barrier = pltpu.get_barrier_semaphore()

    def greet_z(j):
        pl.semaphore_signal(
            barrier, inc=1, device_id={"expert": ring(z + j) * 2 + y}, device_id_type=MESH)

    def greet_other(j):
        pl.semaphore_signal(
            barrier, inc=1, device_id={"section": other, "expert": ring(z + j) * 2 + y},
            device_id_type=MESH)

    each(nz, 1, greet_z)
    each(nz, 0, greet_other)
    pl.semaphore_signal(
        barrier, inc=1, device_id={"expert": z * 2 + 1 - y}, device_id_type=MESH)

    for copy in small:
        copy.wait()
    values = x_ref[0].astype(jnp.float32)
    inv_rms = lax.rsqrt(jnp.mean(values * values, axis=-1, keepdims=True) + epsilon)
    for k in range(na):
        cols = slice(k * ac, (k + 1) * ac)
        gathered[k, rows_at(z), :] = (values[:, cols] * inv_rms * gain_ref[:, cols]).astype(jnp.bfloat16)

    pl.semaphore_wait(barrier, 2 * nz)
    for k in range(na):
        along_y(k, 0).start()
        each(nz, 1, lambda j: along_z(k, j).start())
    res_copy = pltpu.make_async_remote_copy(
        src_ref=x_ref, dst_ref=resid, send_sem=res_sem.at[0], recv_sem=res_sem.at[1],
        device_id={"section": other}, device_id_type=MESH)
    res_copy.start()
    load_gate(slots - 1).start()
    load_up(slots - 1).start()

    def forward(k):
        def one(j):
            from_z(k, j).wait_recv()
            along_y(k, j).start()

        each(nz, 1, one)

    forward(0)
    for k in range(nk):
        if k % per == 0:
            if k // per + 1 < na:
                forward(k // per + 1)
            each(nz, 0, lambda j: along_y(k // per, j).wait_recv())
        load_gate(k).wait()
        load_up(k).wait()
        slot = k % slots

        def tile(t, carry):
            cols = pl.ds(pl.multiple_of(t * ft, ft), ft)
            lhs = gathered[k // per, :, (k % per) * kc:(k % per + 1) * kc]
            gate = jnp.dot(lhs, gate_buf[slot, :, cols], preferred_element_type=jnp.float32)
            up = jnp.dot(lhs, up_buf[slot, :, cols], preferred_element_type=jnp.float32)
            if k > 0:
                gate = gate + gate_acc[:, cols]
                up = up + up_acc[:, cols]
            if k < nk - 1:
                gate_acc[:, cols] = gate
                up_acc[:, cols] = up
            else:
                hidden[:, cols] = (gate / (1.0 + jnp.exp(-gate)) * up).astype(jnp.bfloat16)
            return carry

        lax.fori_loop(0, ff // ft, tile, 0)
        if k + slots < nk:
            load_gate(k + slots).start()
            load_up(k + slots).start()
        first = nk - slots
        if k >= first:
            for c in range(nc * (k - first) // slots, nc * (k - first + 1) // slots):
                load_down(c).start()

    def mix(i, carry):
        side, row = i // nz, lax.rem(i, nz)
        source = row * 2 + jnp.where(side == 0, y, 1 - y)
        here = rows_at(i)
        first = first_col[rows_at(source), 0:1]
        second = second_col[rows_at(source), 0:1]
        first_logit = jnp.zeros((rows, 1), jnp.float32)
        second_logit = jnp.zeros((rows, 1), jnp.float32)
        for e in range(experts):
            logit = logits[here, e:e + 1]
            first_logit = jnp.where(first == e, logit, first_logit)
            second_logit = jnp.where(second == e, logit, second_logit)
        first_gate = 1.0 / (1.0 + jnp.exp(second_logit - first_logit))
        second_gate = 1.0 / (1.0 + jnp.exp(first_logit - second_logit))
        weight = jnp.where(first == expert.astype(jnp.float32), first_gate, 0.0) + jnp.where(
            second == expert.astype(jnp.float32), second_gate, 0.0)
        mixing[here, :] = jnp.broadcast_to(weight, (rows, 128))
        return carry

    ids = routes_ref[...].astype(jnp.float32)
    first_col[...] = jnp.transpose(jnp.broadcast_to(ids[0:1], (8, tokens)))
    second_col[...] = jnp.transpose(jnp.broadcast_to(ids[1:2], (8, tokens)))
    score = jnp.zeros((tokens, experts), jnp.float32)
    for k in range(na):
        rest = router_ref[:, k * ac:(k + 1) * ac]
        for _ in range(3):
            piece = rest.astype(jnp.bfloat16)
            rest = rest - piece.astype(jnp.float32)
            score = score + lax.dot_general(
                gathered[k], piece, (((1,), (1,)), ((), ())), preferred_element_type=jnp.float32)
    logits[:, 0:experts] = score
    lax.fori_loop(0, 2 * nz, mix, 0)

    def second_stage(c):
        reduce_y(c).wait_recv()
        send_z[c] = (own[c] + recv_y[c].astype(jnp.float32)).astype(jnp.bfloat16)
        each(nz, 0, lambda j: reduce_z(c, j).start())

    def down(c, carry):
        load_down(c).wait()
        part = jnp.dot(hidden[...], down_buf[c], preferred_element_type=jnp.float32)
        part = part * mixing[:, 0:1]
        send_y[c] = part[half:].astype(jnp.bfloat16)
        reduce_y(c).start()
        own[c] = part[:half]

        @pl.when(c >= lag)
        def _():
            second_stage(c - lag)

        return carry

    lax.fori_loop(0, nc, down, 0)
    for c in range(nc - lag, nc):
        second_stage(c)
    res_copy.wait_recv()
    for c in range(nc):
        cols = slice(c * cw, (c + 1) * cw)
        each(nz, 0, lambda j: reduce_z(c, j).wait_recv())
        branch = jnp.sum(recv_z[c].astype(jnp.float32), axis=0)
        out_ref[0, :, cols] = (resid[0, :, cols].astype(jnp.float32) + branch).astype(jnp.bfloat16)

    res_copy.wait_send()
    for k in range(na):
        each(nz, 1, lambda j: along_z(k, j).wait_send())
        each(nz, 0, lambda j: along_y(k, j).wait_send())

    def drain(c, carry):
        reduce_y(c).wait_send()
        each(nz, 0, lambda j: reduce_z(c, j).wait_send())
        return carry

    lax.fori_loop(0, nc, drain, 0)


def body(token_rows, norm_gain, router, w_gate, w_up, w_down, routes):
    _, rows, features = token_rows.shape
    ff = w_gate.shape[3]
    experts = router.shape[2]
    nz = lax.axis_size("expert") // 2
    total = 2 * nz * rows
    half = nz * rows
    kc, cw = 512, 512
    nk, nc = features // kc, features // cw
    per, slots, lag = 1, 3, 1
    ft = min(2048, ff)
    cfg = (nz, rows, kc, nk, per, slots, ff, ft, nc, cw, lag, experts)
    vmem = pl.BlockSpec(memory_space=pltpu.VMEM)
    hbm = pl.BlockSpec(memory_space=pl.ANY)
    bf16, f32 = jnp.bfloat16, jnp.float32
    dma = pltpu.SemaphoreType.DMA
    return pl.pallas_call(
        functools.partial(kernel, cfg),
        out_shape=jax.ShapeDtypeStruct((1, rows, features), bf16),
        in_specs=[hbm] * 3 + [vmem] + [hbm] * 3,
        out_specs=vmem,
        scratch_shapes=[
            pltpu.VMEM((1, rows, features), bf16),
            pltpu.VMEM((1, features), f32),
            pltpu.VMEM((experts, features), f32),
            pltpu.VMEM((total, 8), f32),
            pltpu.VMEM((total, 8), f32),
            pltpu.VMEM((total, 8), f32),
            pltpu.VMEM((nk // per, total, kc * per), bf16),
            pltpu.VMEM((slots, kc, ff), bf16),
            pltpu.VMEM((slots, kc, ff), bf16),
            pltpu.VMEM((nc, ff, cw), bf16),
            pltpu.VMEM((total, ff), f32),
            pltpu.VMEM((total, ff), f32),
            pltpu.VMEM((total, ff), bf16),
            pltpu.VMEM((total, 128), f32),
            pltpu.VMEM((nc, half, cw), bf16),
            pltpu.VMEM((nc, half, cw), f32),
            pltpu.VMEM((nc, half, cw), bf16),
            pltpu.VMEM((nc, half, cw), bf16),
            pltpu.VMEM((nc, nz, rows, cw), bf16),
            pltpu.VMEM((1, rows, features), bf16),
            dma((3,)), dma((slots,)), dma((slots,)), dma((nc,)), dma((2,)),
            dma((nk // per, nz)), dma((nk // per, nz)), dma((nk // per, nz)), dma((nk // per, nz)),
            dma((nc,)), dma((nc,)), dma((nc, nz)), dma((nc, nz)),
        ],
        compiler_params=pltpu.CompilerParams(
            collective_id=0, has_side_effects=True, vmem_limit_bytes=62 * 2**20),
    )(token_rows, norm_gain, router[0].T, routes[0].T, w_gate, w_up, w_down)


def solution(mesh):
    in_specs = (
        P("section", ("groups", "expert"), None),
        P("section", None),
        P("section", None, None),
        P("section", "expert", None, None),
        P("section", "expert", None, None),
        P("section", "expert", None, None),
        P("section", "groups", None),
    )
    out_specs = P("section", ("groups", "expert"), None)
    return jax.shard_map(body, mesh=mesh, in_specs=in_specs, out_specs=out_specs, check_vma=False)
```
